32 devices in a mesh: ctx: 8 (over z, core), wt: 4 (over y, x).
Axes of the slice: x: 2, y: 2, z: 4, core: 2. Of those that a mesh axis runs over, the one named last changes fastest.
Arguments:
- tokens: bfloat16 [4, 2048, 1024], P('wt', 'ctx'), may hold values from -6 to 6
- cotangent: bfloat16 [4, 2048, 1024], P('wt', 'ctx'), may hold values from -6 to 6
- ln1_gain: bfloat16 [1024], P('wt'), may hold values from 0.25 to 1.75
- ln1_bias: bfloat16 [1024], P('wt'), may hold values from -3 to 3
- w_qkv: bfloat16 [1024, 3072], P('wt'), may hold values from -0.1875 to 0.1875
- bias_q: bfloat16 [1024], P('wt'), may hold values from -3 to 3
- bias_v: bfloat16 [1024], P('wt'), may hold values from -1.25 to 1.25
- w_out: bfloat16 [1024, 1024], P('wt'), may hold values from -0.75 to 0.75
- bias_out: bfloat16 [1024], P('wt'), may hold values from -3 to 3
- ln2_gain: bfloat16 [1024], P('wt'), may hold values from 0.25 to 1.75
- ln2_bias: bfloat16 [1024], P('wt'), may hold values from -3 to 3
- w_up: bfloat16 [1024, 4096], P('wt'), may hold values from -0.1875 to 0.1875
- bias_up: bfloat16 [4096], P('wt'), may hold values from -3 to 3
- w_down: bfloat16 [4096, 1024], P('wt'), may hold values from -0.09375 to 0.09375
- bias_down: bfloat16 [1024], P('wt'), may hold values from -3 to 3
Outputs:
- out: bfloat16 [4, 2048, 1024], P('wt', 'ctx')
- grad_tokens: float32 [4, 2048, 1024], P('wt', 'ctx')
- grad_ln1_gain: float32 [1024], P('wt')
- grad_ln1_bias: float32 [1024], P('wt')
- grad_w_qkv: float32 [1024, 3072], P('wt')
- grad_bias_q: float32 [1024], P('wt')
- grad_bias_v: float32 [1024], P('wt')
- grad_w_out: float32 [1024, 1024], P('wt')
- grad_bias_out: float32 [1024], P('wt')
- grad_ln2_gain: float32 [1024], P('wt')
- grad_ln2_bias: float32 [1024], P('wt')
- grad_w_up: float32 [1024, 4096], P('wt')
- grad_bias_up: float32 [4096], P('wt')
- grad_w_down: float32 [4096, 1024], P('wt')
- grad_bias_down: float32 [1024], P('wt')
The draws below stay inside these ranges and needn't reach their ends.
All inputs are finite; a program needn't handle non-finite values.
Results may differ from the reference program's by a relative error of at most 0.02.
Values may be sent and summed in bfloat16 or wider, within the bound.
A program may use at most 192 MiB of HBM per device.

```python
from functools import partial
import jax
import jax.numpy as jnp
from jax import lax

D = 1024
HEADS = 16
HEAD_DIM = 64
FF = 4096
TOK_DEV = 256
BLK = 128
LEN = 2048
SEQS = 4
N_CTX = 8


def block_levels(key, dims, split, low, top_value):
    factor_of = 1.0
    for position, blocks in split:
        draws = jax.random.uniform(jax.random.fold_in(jax.random.fold_in(key, 6), position), (blocks,), jnp.float32, low / len(split), top_value / len(split))
        factor_of = factor_of * jnp.repeat(jnp.exp(draws), dims[position] // blocks).reshape((-1,) + (1,) * (len(dims) - 1 - position))
    return factor_of


def noise(key, shape, scale, most, cuts=(), kind=jnp.bfloat16):
    factor_of = block_levels(key, shape, cuts, -0.22, 0.18) if cuts else 1.0
    entries = jax.random.normal(key, shape, jnp.float32) * scale * factor_of
    return jnp.minimum(jnp.maximum(entries, -most), most).astype(kind)


def setup_inputs(seed: int = 0) -> dict:
    key_of = jax.random.split(jax.random.key(seed), 16)
    return {
        "tokens": noise(key_of[0], (SEQS, LEN, D), 1.0, 6.0, ((0, 4), (1, 8))),
        "cotangent": noise(key_of[1], (SEQS, LEN, D), 1.0, 6.0, ((0, 4), (1, 8))),
        "ln1_gain": jnp.clip(1.0 + 0.15 * jax.random.normal(key_of[2], (D,), jnp.float32), 0.25, 1.75).astype(jnp.bfloat16),
        "ln1_bias": noise(key_of[3], (D,), 0.5, 3.0, ((0, 4),)),
        "w_qkv": noise(key_of[4], (D, 3 * D), D ** -0.5, 0.1875, ((0, 4),)),
        "bias_q": noise(key_of[5], (D,), 0.5, 3.0, ((0, 4),)),
        "bias_v": noise(key_of[6], (D,), 0.2, 1.25, ((0, 4),)),
        "w_out": noise(key_of[7], (D, D), (D // 16) ** -0.5, 0.75, ((0, 4),)),
        "bias_out": noise(key_of[8], (D,), 0.5, 3.0, ((0, 4),)),
        "ln2_gain": jnp.clip(1.0 + 0.15 * jax.random.normal(key_of[9], (D,), jnp.float32), 0.25, 1.75).astype(jnp.bfloat16),
        "ln2_bias": noise(key_of[10], (D,), 0.5, 3.0, ((0, 4),)),
        "w_up": noise(key_of[11], (D, FF), D ** -0.5, 0.1875, ((0, 4),)),
        "bias_up": noise(key_of[12], (FF,), 0.5, 3.0, ((0, 4),)),
        "w_down": noise(key_of[13], (FF, D), FF ** -0.5, 0.09375, ((0, 4),)),
        "bias_down": noise(key_of[14], (D,), 0.5, 3.0, ((0, 4),)),
    }


EPSILON = 1e-05
MASKED_SCORE = -1e+30

@jax.custom_vjp
def low(v):
    return lax.optimization_barrier(v.astype(jnp.bfloat16)).astype(jnp.float32)

@jax.custom_vjp
def low_back(v):
    return v

def low_keep(v):
    return (low(v), None)

def low_pass(kept, grad):
    return (grad,)

def back_keep(v):
    return (v, None)

def back_low(kept, grad):
    return (low(grad),)
low.defvjp(low_keep, low_pass)
low_back.defvjp(back_keep, back_low)

def norm_rows(values_in, gain, shift):
    mean_val = lax.optimization_barrier(jnp.mean(values_in, axis=-1, keepdims=True))
    centred = values_in - mean_val
    spread = lax.optimization_barrier(jnp.mean(centred * centred, axis=-1, keepdims=True))
    return centred * lax.rsqrt(spread + EPSILON) * gain + shift

def gelu_tanh(values_in):
    return jax.nn.gelu(values_in, approximate=True)

def product_high(left, right):
    return jnp.dot(left, right, precision=lax.Precision.HIGHEST)

def attention(query_rows, key_rows, value_rows, positions):
    length = query_rows.shape[0]
    block_rows = min(512, length)
    query_blocks = query_rows.reshape(length // block_rows, block_rows, HEADS, HEAD_DIM)
    pos_blocks = positions.reshape(length // block_rows, block_rows)

    def one_block(pair_in):
        query_block, query_pos = pair_in
        scores = jnp.einsum('qhd,khd->hqk', query_block, key_rows, precision=lax.Precision.HIGHEST) * HEAD_DIM ** (-0.5)
        scores = low_back(scores)
        scores = jnp.where(positions[None, None, :] <= query_pos[None, :, None], scores, MASKED_SCORE)
        log_norm = jax.scipy.special.logsumexp(scores, axis=-1, keepdims=True)
        prob_low = low(jnp.exp(scores - log_norm))
        return jnp.einsum('hqk,khd->qhd', prob_low, value_rows, precision=lax.Precision.HIGHEST)
    attended = lax.map(jax.checkpoint(one_block), (query_blocks, pos_blocks))
    return attended.reshape(length, HEADS * HEAD_DIM)

def layer(params, inputs, positions):
    gain_one, shift_one, whole_qkv, query_bias, value_bias, whole_out, out_bias, gain_two, shift_two, whole_up, up_bias, whole_down, down_bias = params
    width = inputs.shape[1]
    normed_one = low(norm_rows(inputs, gain_one, shift_one))
    qkv_bias = jnp.concatenate([query_bias, jnp.zeros_like(query_bias), value_bias])
    qkv_rows = low_back(low(product_high(normed_one, whole_qkv) + qkv_bias))
    query_rows = qkv_rows[:, :width].reshape(-1, HEADS, HEAD_DIM)
    key_rows = qkv_rows[:, width:2 * width].reshape(-1, HEADS, HEAD_DIM)
    value_rows = qkv_rows[:, 2 * width:].reshape(-1, HEADS, HEAD_DIM)
    attended = low_back(low(attention(query_rows, key_rows, value_rows, positions)))
    mixed_attn = low_back(product_high(attended, whole_out) + out_bias)
    resid_mid = inputs + mixed_attn
    normed_two = low(norm_rows(resid_mid, gain_two, shift_two))
    hidden_pre = low_back(product_high(normed_two, whole_up) + up_bias)
    hidden_low = low(gelu_tanh(hidden_pre))
    return resid_mid + product_high(hidden_low, whole_down) + down_bias

def reference(tokens, cotangent, ln1_gain, ln1_bias, w_qkv, bias_q, bias_v, w_out, bias_out, ln2_gain, ln2_bias, w_up, bias_up, w_down, bias_down):
    rows_all = jnp.arange(LEN, dtype=jnp.int32)
    device_of = rows_all // TOK_DEV
    half_of = rows_all // BLK % 2
    block_of = jnp.where(half_of == 0, device_of, 2 * N_CTX - 1 - device_of)
    positions = (block_of * BLK + rows_all % BLK).astype(jnp.int32)
    params = tuple((weight.astype(jnp.float32) for weight in (ln1_gain, ln1_bias, w_qkv, bias_q, bias_v, w_out, bias_out, ln2_gain, ln2_bias, w_up, bias_up, w_down, bias_down)))
    forward = partial(layer, positions=positions)

    def one_sequence(totals, pair_in):
        seq_tokens, seq_grad = pair_in
        result, pullback = jax.vjp(forward, params, seq_tokens.astype(jnp.float32))
        grad_params, grad_inputs = pullback(seq_grad.astype(jnp.float32))
        totals = jax.tree.map(jnp.add, totals, grad_params)
        return (totals, (result.astype(jnp.bfloat16), grad_inputs))
    initial = tuple((jnp.zeros_like(weight) for weight in params))
    totals, (out, grad_tokens) = lax.scan(one_sequence, initial, (tokens, cotangent))
    return (out, grad_tokens, totals[0], totals[1], totals[2], totals[3], totals[4], totals[5], totals[6], totals[7], totals[8], totals[9], totals[10], totals[11], totals[12])
```

```python
import functools

import jax
import jax.numpy as jnp
import numpy as np
from jax import lax
from jax.experimental import pallas as pl
from jax.experimental.pallas import tpu as pltpu
from jax.sharding import Mesh
from jax.sharding import PartitionSpec as P

HEADS = 16
HEAD_DIM = 64


EPSILON = 1e-05
MASKED_SCORE = -1e30
Q_TILE = 256
K_TILE = 512


def norm_rows(values_in, gain, shift):
    mean_val = jnp.mean(values_in, axis=-1, keepdims=True)
    centred = values_in - mean_val
    spread = jnp.mean(centred * centred, axis=-1, keepdims=True)
    return centred * lax.rsqrt(spread + EPSILON) * gain + shift


def gelu_tanh(values_in):
    return jax.nn.gelu(values_in, approximate=True)


def product(left, right):
    return jnp.dot(left, right, preferred_element_type=jnp.float32)


def product_left(left, right):
    return lax.dot_general(
        left, right, (((0,), (0,)), ((), ())), preferred_element_type=jnp.float32
    )


def product_right(left, right):
    return lax.dot_general(
        left, right, (((1,), (1,)), ((), ())), preferred_element_type=jnp.float32
    )


def tile_allowed(q_start, k_start):
    q_pos = q_start + lax.broadcasted_iota(jnp.int32, (Q_TILE, K_TILE), 0)
    k_pos = k_start + lax.broadcasted_iota(jnp.int32, (Q_TILE, K_TILE), 1)
    return k_pos <= q_pos


def remote(src, dst, send_sem, recv_sem, **where):
    return pltpu.make_async_remote_copy(
        src_ref=src,
        dst_ref=dst,
        send_sem=send_sem,
        recv_sem=recv_sem,
        device_id=where,
        device_id_type=pl.DeviceIdType.MESH,
    )


def greet(targets):
    barrier = pltpu.get_barrier_semaphore()
    for where in targets:
        pl.semaphore_signal(
            barrier, inc=1, device_id=where, device_id_type=pl.DeviceIdType.MESH
        )
    pl.semaphore_wait(barrier, len(targets))


def all_peers(shards, chips, me, z, core):
    return (
        [{"wt": lax.rem(me + k, shards)} for k in range(1, shards)]
        + [{"z": lax.rem(z + k, chips)} for k in range(1, chips)]
        + [{"core": 1 - core}]
    )


class Gather:
    def __init__(self, ref, own, sends, recvs, base, shards, me):
        self.own = own
        self.ref, self.sends, self.recvs, self.base = ref, sends, recvs, base
        self.shards, self.me, self.outer = shards, me, shards // 2
        self.a, self.b = me // 2, lax.rem(me, 2)
        self.half = ref.shape[1] // 2
        self.partner = self.a * 2 + 1 - self.b

    @staticmethod
    def count(shards):
        return 1 + 3 * (shards // 2 - 1)

    def part(self, slot, which):
        return self.ref.at[slot, pl.ds(which * self.half, self.half)]

    def column(self, k):
        return lax.rem(self.a + k, self.outer) * 2 + self.b

    def copy(self, ref, sem, wt, own=None):
        return remote(ref if own is None else own, ref, self.sends.at[sem], self.recvs.at[sem], wt=wt)

    def direct(self):
        mine = self.ref.at[self.me]
        steps = [self.copy(mine, self.base, self.partner, self.own)]
        for k in range(1, self.outer):
            steps.append(self.copy(mine, self.base + k, self.column(k), self.own))
        return steps

    def relays(self):
        first, second = [], []
        for k in range(1, self.outer):
            first.append(
                self.copy(self.part(self.partner, 0), self.base + self.outer - 1 + k, self.column(k))
            )
            second.append(
                self.copy(
                    self.part(self.column(self.outer - k), 1),
                    self.base + 2 * (self.outer - 1) + k,
                    self.partner,
                )
            )
        return first, second

    def start(self):
        for step in self.direct():
            step.start()

    def relay(self):
        first, second = self.relays()
        self.copy(self.ref.at[self.partner], self.base, self.partner).wait_recv()
        for step in first:
            step.start()
        for k in range(1, self.outer):
            slot = self.column(self.outer - k)
            self.copy(self.ref.at[slot], self.base + k, slot).wait_recv()
            second[k - 1].start()

    def near(self):
        return [self.partner] + [self.column(k) for k in range(1, self.outer)]

    def landed(self):
        for n, slot in enumerate([self.partner] + [self.column(self.outer - k) for k in range(1, self.outer)]):
            self.copy(self.ref.at[slot], self.base + n, self.partner).wait_recv()

    def pass_on(self):
        first, second = self.relays()
        for step in first + second:
            step.start()

    def passed_on(self):
        first, second = self.relays()
        for step in first + second:
            step.wait_send()

    def arrived(self):
        for k in range(1, self.outer):
            slot = lax.rem(self.a + self.outer - k, self.outer) * 2 + 1 - self.b
            self.copy(self.part(slot, 0), self.base + self.outer - 1 + k, self.partner).wait_recv()
            self.copy(
                self.part(slot, 1), self.base + 2 * (self.outer - 1) + k, self.partner
            ).wait_recv()

    def sent(self):
        first, second = self.relays()
        for step in self.direct() + first + second:
            step.wait_send()


VEC_ROWS = 16


def wide_row(vecs, row, shards):
    return jnp.concatenate([vecs[s, row : row + 1, :] for s in range(shards)], axis=1)


def forward_kernel(
    shards,
    chips,
    heads,
    tokens,
    vec,
    own_qkv,
    w_out,
    w_up,
    w_down,
    vecs,
    h1,
    qkv,
    att,
    lse,
    att_low,
    g_qkv,
    g_out,
    g_up,
    g_down,
    att_send,
    s_out,
    s_up,
    s_down,
    wt_send,
    wt_recv,
    vec_send,
    vec_recv,
    z_send,
    z_recv,
    sib_send,
    sib_recv,
    tile_send,
    tile_recv,
    local,
):
    me, z, core = lax.axis_index("wt"), lax.axis_index("z"), lax.axis_index("core")
    devices = 2 * chips
    cols = heads * HEAD_DIM
    rows, width = tokens.shape
    block = rows // 2
    per = Gather.count(shards)
    gathers = [
        Gather(ref, own, wt_send, wt_recv, per * i, shards, me)
        for i, (ref, own) in enumerate(
            ((g_qkv, own_qkv), (g_out, s_out), (g_up, s_up), (g_down, s_down))
        )
    ]

    vecs[me] = vec[...]
    g_qkv[me] = own_qkv[...]
    stage = []
    groups = w_out.shape[0] // (2 * cols)
    for g in range(groups):
        stage.append(
            pltpu.make_async_copy(
                w_out.at[pl.ds(g * 2 * cols + core * cols, cols)],
                s_out.at[pl.ds(g * cols, cols)],
                local.at[g],
            )
        )
    share = w_up.shape[1] // shards // 2
    for s in range(shards):
        stage.append(
            pltpu.make_async_copy(
                w_up.at[:, pl.ds(s * 2 * share + core * share, share)],
                s_up.at[:, pl.ds(s * share, share)],
                local.at[groups + s],
            )
        )
    down = w_down.shape[0] // 2
    stage.append(
        pltpu.make_async_copy(
            w_down.at[pl.ds(core * down, down)], s_down, local.at[groups + shards]
        )
    )
    for step in stage:
        step.start()
    greet(all_peers(shards, chips, me, z, core))
    vec_steps = [
        remote(
            vecs.at[me], vecs.at[me], vec_send.at[k], vec_recv.at[k], wt=lax.rem(me + k, shards)
        )
        for k in range(1, shards)
    ]
    for step in vec_steps:
        step.start()
    gathers[0].start()
    for step in stage[:groups]:
        step.wait()
    gathers[1].start()
    for step in stage[groups : groups + shards]:
        step.wait()
    gathers[2].start()
    stage[-1].wait()
    keep = [
        pltpu.make_async_copy(own, ref.at[me], local.at[groups + shards + 1 + i])
        for i, (own, ref) in enumerate(((s_out, g_out), (s_up, g_up), (s_down, g_down)))
    ]
    for step in keep:
        step.start()

    values_in = tokens[...].astype(jnp.float32)
    centred = values_in - jnp.mean(values_in, axis=-1, keepdims=True)
    spread = jnp.mean(centred * centred, axis=-1, keepdims=True)
    scaled = centred * lax.rsqrt(spread + EPSILON)
    for k in range(1, shards):
        slot = lax.rem(me + shards - k, shards)
        remote(vecs.at[slot], vecs.at[slot], vec_send.at[k], vec_recv.at[k], wt=slot).wait_recv()
    mine = z * 2 + core
    h1[mine] = (scaled * wide_row(vecs, 0, shards) + wide_row(vecs, 1, shards)).astype(
        jnp.bfloat16
    )

    def right(slot, d):
        return remote(h1.at[slot], h1.at[slot], z_send.at[0, d], z_recv.at[0, d], z=z + 1)

    def left(slot, d):
        return remote(h1.at[slot], h1.at[slot], z_send.at[1, d], z_recv.at[1, d], z=z - 1)

    def sibling(chip, of):
        slot = chip * 2 + of
        return remote(
            h1.at[slot], h1.at[slot], sib_send.at[chip], sib_recv.at[chip], core=1 - core
        )

    @pl.when(z + 1 < chips)
    def _():
        right(mine, 1).start()

    @pl.when(z > 0)
    def _():
        left(mine, 1).start()

    sibling(z, core).start()
    gathers[0].relay()
    gathers[0].arrived()
    gathers[3].start()

    per_shard = vecs.shape[2] // cols
    group = z * 2 + core
    bias_shard, bias_row = group // per_shard, lax.rem(group, per_shard)
    bias_q = vecs[bias_shard, pl.ds(10 + bias_row, 1), :][:, :cols]
    bias_v = vecs[bias_shard, pl.ds(10 + per_shard + bias_row, 1), :][:, :cols]
    bias = jnp.concatenate([bias_q, jnp.zeros_like(bias_q), bias_v], axis=1)

    def project(slot):
        whole = g_qkv[...].reshape(width, 3 * cols)
        result = (product(h1[slot], whole) + bias).astype(jnp.bfloat16)
        qkv[pl.ds(slot * block, block), :] = result[:block]
        qkv[pl.ds((2 * devices - 1 - slot) * block, block), :] = result[block:]

    sibling(z, 1 - core).wait_recv()

    @pl.loop(0, 2)
    def _(i):
        project(z * 2 + i)

    for d in range(1, chips):

        @pl.when(z >= d)
        def _():
            chip = z - d
            slot = chip * 2 + core
            right(slot, d).wait_recv()

            @pl.when(z + 1 < chips)
            def _():
                right(slot, d + 1).start()

            sibling(chip, core).start()

        @pl.when(z + d < chips)
        def _():
            chip = z + d
            slot = chip * 2 + core
            left(slot, d).wait_recv()

            @pl.when(z > 0)
            def _():
                left(slot, d + 1).start()

            sibling(chip, core).start()

        if d == 1:
            gathers[1].relay()

        @pl.loop(0, 2)
        def _(i):
            chip = jnp.where(i == 0, z - d, z + d)

            @pl.when((chip >= 0) & (chip < chips))
            def _():
                project(chip * 2 + core)
                sibling(chip, 1 - core).wait_recv()
                project(chip * 2 + 1 - core)

    gathers[2].relay()

    scale = HEAD_DIM ** (-0.5)
    tiles = 2 * chips

    def tile_copies(i):
        low = i < chips
        chip = jnp.where(low, i, tiles - 1 - i)
        places = [jnp.where(low, 0, 3), jnp.where(low, 2, 1)]
        return chip, places, [
            remote(
                att_send.at[i, pl.ds(j * block, block)],
                att_low.at[z, pl.ds(places[j] * block, block)],
                tile_send.at[i, j],
                tile_recv.at[z, places[j]],
                z=chip,
            )
            for j in range(2)
        ]

    @pl.loop(0, tiles)
    def _(i):
        q_start = pl.multiple_of(i * Q_TILE, Q_TILE)
        q_rows = pl.ds(q_start, Q_TILE)
        queries = [
            qkv[q_rows, h * HEAD_DIM : (h + 1) * HEAD_DIM] * jnp.bfloat16(scale)
            for h in range(heads)
        ]

        def step(masked, j, carried):
            k_start = pl.multiple_of(j * K_TILE, K_TILE)
            k_rows = pl.ds(k_start, K_TILE)
            new = []
            for h in range(heads):
                peak, total, acc = carried[h]
                at = cols + h * HEAD_DIM
                keys = qkv[k_rows, at : at + HEAD_DIM]
                values = qkv[k_rows, at + cols : at + cols + HEAD_DIM]
                scores = product_right(queries[h], keys)
                if masked:
                    scores = jnp.where(tile_allowed(q_start, k_start), scores, MASKED_SCORE)
                peak_new = jnp.maximum(peak, jnp.max(scores, axis=-1, keepdims=True))
                fade = jnp.exp(peak - peak_new)
                prob = jnp.exp(scores - peak_new)
                total = total * fade + jnp.sum(prob, axis=-1, keepdims=True)
                acc = acc * fade + product(prob.astype(jnp.bfloat16), values)
                new.append((peak_new, total, acc))
            return tuple(new)

        empty = (
            jnp.full((Q_TILE, 1), MASKED_SCORE, jnp.float32),
            jnp.zeros((Q_TILE, 1), jnp.float32),
            jnp.zeros((Q_TILE, HEAD_DIM), jnp.float32),
        )
        steps = (q_start + Q_TILE + K_TILE - 1) // K_TILE
        done = lax.fori_loop(
            0, steps - 1, functools.partial(step, False), (empty,) * heads
        )
        done = step(True, steps - 1, done)
        for h in range(heads):
            peak, total, acc = done[h]
            result = acc / total
            att[q_rows, h * HEAD_DIM : (h + 1) * HEAD_DIM] = result
            att_send[i, :, h * HEAD_DIM : (h + 1) * HEAD_DIM] = result.astype(jnp.bfloat16)
            lse[q_rows, h : h + 1] = peak + jnp.log(total)
        chip, places, copies = tile_copies(i)

        @pl.when(chip != z)
        def _():
            for copy in copies:
                copy.start()

        @pl.when(chip == z)
        def _():
            for j in range(2):
                at = pl.multiple_of(places[j] * block, block)
                att_low[z, pl.ds(at, block)] = att_send[i, j * block : (j + 1) * block]

    gathers[3].landed()
    for gather in gathers[1:3]:
        gather.arrived()
    for gather in gathers[:3]:
        gather.sent()
    for step in gathers[3].direct():
        step.wait_send()
    for step in vec_steps:
        step.wait_send()
    for step in keep:
        step.wait()

    @pl.loop(0, tiles)
    def _(i):
        chip, places, copies = tile_copies(i)

        @pl.when(chip != z)
        def _():
            for copy in copies:
                copy.wait_send()

    @pl.loop(0, chips)
    def _(chip):
        sibling(chip, core).wait_send()

        @pl.when(chip != z)
        def _():
            for place in range(4):
                ref = att_low.at[chip, pl.ds(place * block, block)]
                remote(ref, ref, tile_send.at[0, 0], tile_recv.at[chip, place], z=chip).wait_recv()

    for d in range(1, chips + 1):

        @pl.when((z + 1 < chips) & (z - d + 1 >= 0))
        def _():
            right((z - d + 1) * 2 + core, d).wait_send()

        @pl.when((z > 0) & (z + d - 1 < chips))
        def _():
            left((z + d - 1) * 2 + core, d).wait_send()


def forward(tokens, vec, own_qkv, w_out, w_up, w_down, shards, chips, heads):
    rows, width = tokens.shape
    cols = heads * HEAD_DIM
    length = 2 * chips * rows
    tiles = length // Q_TILE
    per = Gather.count(shards)
    vmem = pl.BlockSpec(memory_space=pltpu.VMEM)
    hbm = pl.BlockSpec(memory_space=pl.ANY)
    low, full = jnp.bfloat16, jnp.float32
    shape = jax.ShapeDtypeStruct
    groups = w_out.shape[0] // (2 * cols)
    dma = pltpu.SemaphoreType.DMA
    return pl.pallas_call(
        functools.partial(forward_kernel, shards, chips, heads),
        in_specs=[vmem, vmem, vmem, hbm, hbm, hbm],
        out_specs=[vmem] * 7 + [hbm] * 3,
        out_shape=[
            shape((shards,) + vec.shape, full),
            shape((2 * chips, rows, width), low),
            shape((length, 3 * cols), low),
            shape((length, cols), full),
            shape((length, heads), full),
            shape((chips, 2 * rows, cols), low),
            shape((shards,) + own_qkv.shape, low),
            shape((shards, w_out.shape[0] // 2, width), low),
            shape((shards, w_up.shape[0], w_up.shape[1] // 2), low),
            shape((shards, w_down.shape[0] // 2, width), low),
        ],
        scratch_shapes=[
            pltpu.VMEM((tiles, Q_TILE, cols), low),
            pltpu.VMEM((w_out.shape[0] // 2, width), low),
            pltpu.VMEM((w_up.shape[0], w_up.shape[1] // 2), low),
            pltpu.VMEM((w_down.shape[0] // 2, width), low),
            dma((4 * per,)),
            dma((4 * per,)),
            dma((shards,)),
            dma((shards,)),
            dma((2, chips + 1)),
            dma((2, chips + 1)),
            dma((chips,)),
            dma((chips,)),
            dma((tiles, 2)),
            dma((chips, 4)),
            dma((4 + groups + shards,)),
        ],
        compiler_params=pltpu.CompilerParams(
            vmem_limit_bytes=48 << 20, collective_id=0, has_side_effects=True
        ),
        cost_estimate=pl.CostEstimate(
            flops=20 << 30, bytes_accessed=50 << 20, transcendentals=length * length
        ),
    )(tokens, vec, own_qkv, w_out, w_up, w_down)


def add_rows(dst, sources, step=64):
    rows = dst.shape[0]
    step = min(step, rows)

    @pl.loop(0, rows // step)
    def _(i):
        at = pl.ds(pl.multiple_of(i * step, step), step)
        total = dst[at].astype(jnp.float32)
        for source in sources:
            total = total + source[at].astype(jnp.float32)
        dst[at] = total.astype(dst.dtype)


class Counter:
    def __init__(self, sends, recvs):
        self.sends, self.recvs, self.used = sends, recvs, 0

    def take(self, count=1):
        at = self.used
        self.used += count
        return at


class Scatter:
    @staticmethod
    def scratch(outer, rows, columns):
        low = jnp.bfloat16
        half = rows // 2
        return [
            pltpu.VMEM((rows, columns), low),
            pltpu.VMEM((half, columns), low),
            pltpu.VMEM((outer - 1, half, columns), low),
            pltpu.VMEM((outer - 1, half, columns), low),
            pltpu.VMEM((outer - 1, half, columns), low),
            pltpu.VMEM((rows, columns), low),
            pltpu.VMEM((outer - 1, rows, columns), low),
        ]

    @staticmethod
    def count(outer):
        return 2 + 4 * (outer - 1) + (outer - 1)

    def __init__(self, part, bufs, ids, loads, shards, me):
        self.part, self.loads = part, loads
        self.mine, self.px, self.py, self.yd, self.xd, self.x2, self.y2 = bufs
        self.ids, self.me, self.outer = ids, me, shards // 2
        self.a, self.b = me // 2, lax.rem(me, 2)
        self.half = part.shape[1] // 2
        self.partner = self.a * 2 + 1 - self.b
        far = self.outer - 1
        self.s_yd = ids.take(far)
        self.s_xd = ids.take(far)
        self.s_x2 = ids.take(2)
        self.s_y2 = ids.take(2 * far)

    def column(self, k):
        return lax.rem(self.a + k, self.outer) * 2 + self.b

    def diagonal(self, k):
        return lax.rem(self.a + k, self.outer) * 2 + 1 - self.b

    def send(self, src, dst, sem, wt):
        return remote(src, dst, self.ids.sends.at[sem], self.ids.recvs.at[sem], wt=wt)

    def piece(self, slot, which):
        return self.part.at[slot, pl.ds(which * self.half, self.half)]

    def local_copies(self):
        pairs = [
            (self.part.at[self.me], self.mine),
            (self.piece(self.partner, 0), self.px),
        ] + [(self.piece(self.column(k), 1), self.py.at[k - 1]) for k in range(1, self.outer)]
        return [
            pltpu.make_async_copy(src, dst, self.loads.at[i]) for i, (src, dst) in enumerate(pairs)
        ]

    def first(self):
        steps = []
        for k in range(1, self.outer):
            slot = self.diagonal(k)
            steps.append(
                self.send(
                    self.piece(slot, 0), self.yd.at[k - 1], self.s_yd + k - 1, self.column(k)
                )
            )
            steps.append(
                self.send(
                    self.piece(slot, 1), self.xd.at[k - 1], self.s_xd + k - 1, self.partner
                )
            )
        return steps

    def early(self):
        top, low = pl.ds(0, self.half), pl.ds(self.half, self.half)
        steps = [self.send(self.piece(self.partner, 1), self.x2.at[low], self.s_x2, self.partner)]
        for k in range(1, self.outer):
            slot = self.column(k)
            steps.append(
                self.send(
                    self.piece(slot, 0), self.y2.at[k - 1, top], self.s_y2 + 2 * (k - 1), slot
                )
            )
        return steps

    def late(self):
        top, low = pl.ds(0, self.half), pl.ds(self.half, self.half)
        steps = [self.send(self.px, self.x2.at[top], self.s_x2 + 1, self.partner)]
        for k in range(1, self.outer):
            steps.append(
                self.send(
                    self.py.at[k - 1],
                    self.y2.at[k - 1, low],
                    self.s_y2 + 2 * (k - 1) + 1,
                    self.column(k),
                )
            )
        return steps

    def start_first(self):
        for step in self.first():
            step.start()

    def start_early(self):
        for step in self.early():
            step.start()

    def start_late(self):
        for step in self.local_copies():
            step.wait()
        for step in self.first():
            step.wait_recv()
        add_rows(self.px, [self.yd.at[k] for k in range(self.outer - 1)])
        for k in range(self.outer - 1):
            add_rows(self.py.at[k], [self.xd.at[k]])
        for step in self.late():
            step.start()

    def finish(self):
        for step in self.early() + self.late():
            step.wait_recv()
        add_rows(self.mine, [self.x2] + [self.y2.at[k] for k in range(self.outer - 1)])

    def sent(self):
        for step in self.first() + self.early() + self.late():
            step.wait_send()


class Chain:
    def __init__(self, own, inbox, total, ids, pieces, chips, z, core):
        self.own, self.inbox, self.total, self.ids = own, inbox, total, ids
        self.pieces, self.chips, self.z, self.core = pieces, chips, z, core
        self.rows = own.shape[0] // (2 * pieces)
        self.base = ids.take(6 * pieces)

    def parts(self, way, j):
        at = pl.ds(pl.multiple_of((way * self.pieces + j) * self.rows, self.rows), self.rows)
        ahead = self.z - 1 if way else self.z + 1
        behind = self.z + 1 if way else self.z - 1
        base = self.base + 3 * (way * self.pieces + j)
        sends, recvs = self.ids.sends, self.ids.recvs
        done = self.total.at[self.core, at]
        forth = remote(
            self.own.at[at], self.inbox.at[at], sends.at[base], recvs.at[base], z=ahead
        )
        back = remote(done, done, sends.at[base + 1], recvs.at[base + 1], z=behind)
        aside = remote(
            done, done, sends.at[base + 2], recvs.at[base + 2], core=1 - self.core
        )
        return at, forth, back, aside

    def hops(self, way):
        return self.chips - 1 - self.z if way else self.z

    def waves(self):
        return 2 * (self.chips - 1) + self.pieces

    def wave(self, turn):
        end = self.chips - 1
        for way in range(2):
            hops = self.hops(way)
            out = turn - hops

            @pl.when((out >= 0) & (out < self.pieces))
            def _():
                at, forth, back, aside = self.parts(way, out)

                @pl.when(hops > 0)
                def _():
                    forth.wait_recv()
                    add_rows(self.own.at[at], [self.inbox.at[at]])

                @pl.when(hops == end)
                def _():
                    self.total[self.core, at] = self.own[at]
                    back.start()
                    aside.start()

                @pl.when(hops < end)
                def _():
                    forth.start()

            home = turn - 2 * end + hops

            @pl.when((home >= 0) & (home < self.pieces) & (hops < end))
            def _():
                _, _, back, aside = self.parts(way, home)
                back.wait_recv()
                aside.start()

                @pl.when(hops > 0)
                def _():
                    back.start()

    def finish(self):
        end = self.chips - 1

        @pl.loop(0, self.pieces)
        def _(j):
            for way in range(2):
                hops = self.hops(way)
                at, forth, back, aside = self.parts(way, j)
                base = self.base + 3 * (way * self.pieces + j)
                theirs = self.total.at[1 - self.core, at]
                remote(
                    theirs,
                    theirs,
                    self.ids.sends.at[base + 2],
                    self.ids.recvs.at[base + 2],
                    core=1 - self.core,
                ).wait_recv()
                aside.wait_send()

                @pl.when(hops < end)
                def _():
                    forth.wait_send()

                @pl.when(hops > 0)
                def _():
                    back.wait_send()


PIECES = (4, 4, 2)
LINE_CUTS = 2


FF_TILE = 256


def feed_kernel(shards, chips, *refs):
    refs = list(refs)

    def take(count):
        got = refs[:count]
        del refs[:count]
        return got

    (att_low, w_out, far_up, far_down, tokens, cotangent) = take(6)
    (out_bias, gain, shift, down_bias, up_bias) = take(5)
    (out, grad_mid, pair_z, grad_up, grad_out, red_down, sums, up_sums) = take(8)
    bufs = take(7)
    (w_up, w_down, pair_g, pair_h, turned, p_down, normal, resid) = take(8)
    (down_acc, back_acc, swap_out, swap_in, sends, recvs, loads) = take(7)

    me, z, core = lax.axis_index("wt"), lax.axis_index("z"), lax.axis_index("core")
    outer = shards // 2
    cols = att_low.shape[2]
    rows, width = tokens.shape
    other = 1 - core
    ids = Counter(sends, recvs)
    per_load = 1 + outer
    scatter = Scatter(p_down, bufs, ids, loads.at[pl.ds(0, per_load)], shards, me)
    base = ids.take(6)
    share = p_down.shape[1]
    gather = Gather(w_down, None, sends, recvs, ids.take(Gather.count(shards)), shards, me)

    def cross(src, dst, n):
        return remote(src, dst, sends.at[base + n], recvs.at[base + n], core=other)

    up_load = pltpu.make_async_copy(far_up, w_up, loads.at[per_load])
    down_loads = [
        pltpu.make_async_copy(far_down.at[slot], w_down.at[slot], loads.at[per_load + 1 + n])
        for n, slot in enumerate([me] + gather.near())
    ]
    for step in down_loads:
        step.start()
    up_load.start()
    greet(
        [{"wt": lax.rem(me + k, shards)} for k in range(1, shards)] + [{"core": other}]
    )
    pair_g[core] = cotangent[...]
    give_g = cross(pair_g.at[core], pair_g.at[core], 0)
    give_g.start()
    for step in down_loads:
        step.wait()
    gather.pass_on()

    def mixed(which):
        at = pl.ds(pl.multiple_of(which * rows, rows), rows)
        total = jnp.zeros((rows, width), jnp.float32)
        for chip in range(chips):
            total = total + product(
                att_low[chip, at, :], w_out[chip * cols : (chip + 1) * cols, :]
            )
        return total

    swap_out[0] = mixed(other).astype(jnp.bfloat16)
    give_mix = cross(swap_out.at[0], swap_in.at[0], 1)
    give_mix.start()
    x2 = tokens[...].astype(jnp.float32) + mixed(core)
    give_mix.wait_recv()
    x2 = x2 + swap_in[0].astype(jnp.float32) + out_bias[...]
    resid[...] = x2
    centred = x2 - jnp.mean(x2, axis=-1, keepdims=True)
    spread = lax.rsqrt(jnp.mean(centred * centred, axis=-1, keepdims=True) + EPSILON)
    normal[...] = centred * spread
    pair_h[core] = (centred * spread * gain[...] + shift[...]).astype(jnp.bfloat16)
    give_h = cross(pair_h.at[core], pair_h.at[core], 2)
    give_h.start()
    down_acc[...] = jnp.zeros_like(down_acc)
    back_acc[...] = jnp.zeros_like(back_acc)
    up_load.wait()
    cross(pair_g.at[other], pair_g.at[other], 0).wait_recv()
    cross(pair_h.at[other], pair_h.at[other], 2).wait_recv()
    turned[...] = pair_h[...].reshape(2 * rows, width).T
    gather.arrived()

    order = [scatter.diagonal(k) for k in range(1, outer)]
    order += [scatter.partner] + [scatter.column(k) for k in range(1, outer)] + [me]
    tiles = share // FF_TILE

    @pl.loop(0, shards * tiles)
    def _(i):
        turn, tile = i // tiles, lax.rem(i, tiles)
        slot = jnp.int32(0)
        for n, which in enumerate(order):
            slot = jnp.where(turn == n, which, slot)
        at = pl.ds(pl.multiple_of(slot * share + tile * FF_TILE, FF_TILE), FF_TILE)
        down_at = pl.ds(pl.multiple_of(tile * FF_TILE, FF_TILE), FF_TILE)
        g = pair_g[...].reshape(2 * rows, width)
        u = product(pair_h[...].reshape(2 * rows, width), w_up[:, at]) + up_bias[:, at]
        da = product_right(g, w_down[slot, down_at, :])
        cube = 0.044715 * u * u
        slope = 0.7978845608028654
        bend = jnp.tanh(slope * u * (1.0 + cube))
        half = 0.5 * (1.0 + bend)
        act = (u * half).astype(jnp.bfloat16)
        rise = half + 0.5 * u * (1.0 - bend * bend) * slope * (1.0 + 3.0 * cube)
        du = (da * rise).astype(jnp.bfloat16)
        p_down[slot, pl.ds(pl.multiple_of(tile * FF_TILE, FF_TILE), FF_TILE), :] = product_left(
            act, g
        ).astype(jnp.bfloat16)
        grad_up[:, at] = product(turned[...], du).astype(jnp.bfloat16)
        up_sums[:, at] = jnp.sum(du.astype(jnp.float32), axis=0, keepdims=True)
        down_acc[...] += product(act, w_down[slot, down_at, :])
        back_acc[...] += product_right(du, w_up[:, at])

        @pl.when(i == (outer - 1) * tiles - 1)
        def _():
            scatter.start_first()

        @pl.when(i == (2 * outer - 1) * tiles - 1)
        def _():
            scatter.start_early()

    for step in scatter.local_copies():
        step.start()
    their = pl.ds(pl.multiple_of(other * rows, rows), rows)
    own = pl.ds(pl.multiple_of(core * rows, rows), rows)
    swap_out[1] = back_acc[their, :].astype(jnp.bfloat16)
    give_back = cross(swap_out.at[1], swap_in.at[1], 3)
    give_back.start()
    swap_out[2] = down_acc[their, :].astype(jnp.bfloat16)
    give_down = cross(swap_out.at[2], swap_in.at[2], 4)
    give_down.start()
    scatter.start_late()
    g_own = cotangent[...].astype(jnp.float32)
    give_back.wait_recv()
    dh2 = back_acc[own, :] + swap_in[1].astype(jnp.float32)
    xh = normal[...]
    inner = dh2 * gain[...]
    x2 = resid[...]
    centred = x2 - jnp.mean(x2, axis=-1, keepdims=True)
    spread = lax.rsqrt(jnp.mean(centred * centred, axis=-1, keepdims=True) + EPSILON)
    dx2 = g_own + spread * (
        inner
        - jnp.mean(inner, axis=-1, keepdims=True)
        - xh * jnp.mean(inner * xh, axis=-1, keepdims=True)
    )
    grad_mid[...] = dx2
    dz = dx2.astype(jnp.bfloat16)
    pair_z[core] = dz
    give_z = cross(pair_z.at[core], pair_z.at[core], 5)
    give_z.start()
    sums[...] = jnp.concatenate(
        [
            jnp.sum(dz.astype(jnp.float32), axis=0, keepdims=True),
            jnp.sum(dh2 * xh, axis=0, keepdims=True),
            jnp.sum(dh2, axis=0, keepdims=True),
            jnp.sum(g_own, axis=0, keepdims=True),
            jnp.zeros((4, width), jnp.float32),
        ]
    )
    give_down.wait_recv()
    out[...] = (
        x2 + down_acc[own, :] + swap_in[2].astype(jnp.float32) + down_bias[...]
    ).astype(jnp.bfloat16)
    cross(pair_z.at[other], pair_z.at[other], 5).wait_recv()
    pair = pair_z[...].reshape(2 * rows, width)
    for chip in range(chips):
        grad_out[chip * cols : (chip + 1) * cols, :] = product_left(att_low[chip], pair).astype(
            jnp.bfloat16
        )
    scatter.finish()
    red_down[...] = bufs[0][...]
    scatter.sent()
    gather.passed_on()
    for step in (give_g, give_mix, give_h, give_back, give_down, give_z):
        step.wait_send()


def feed(att_low, w_out, w_up, w_down, tokens, cotangent, biases, shards, chips):
    rows, width = tokens.shape
    hidden = w_up.shape[1]
    outer = shards // 2
    vmem = pl.BlockSpec(memory_space=pltpu.VMEM)
    hbm = pl.BlockSpec(memory_space=pl.ANY)
    low, full = jnp.bfloat16, jnp.float32
    shape = jax.ShapeDtypeStruct
    dma = pltpu.SemaphoreType.DMA
    down = (hidden // shards, width)
    sems = 2 + 4 * (outer - 1) + 6 + Gather.count(shards)
    return pl.pallas_call(
        functools.partial(feed_kernel, shards, chips),
        in_specs=[vmem, vmem, hbm, hbm] + [vmem] * 7,
        out_specs=[vmem] * 8,
        out_shape=[
            shape((rows, width), low),
            shape((rows, width), full),
            shape((2, rows, width), low),
            shape((width, hidden), low),
            shape((width // 2, width), low),
            shape(down, low),
            shape((8, width), full),
            shape((1, hidden), full),
        ],
        scratch_shapes=Scatter.scratch(outer, *down)
        + [
            pltpu.VMEM((width, hidden), low),
            pltpu.VMEM(w_down.shape, low),
            pltpu.VMEM((2, rows, width), low),
            pltpu.VMEM((2, rows, width), low),
            pltpu.VMEM((width, 2 * rows), low),
            pltpu.VMEM((shards,) + down, low),
            pltpu.VMEM((rows, width), full),
            pltpu.VMEM((rows, width), full),
            pltpu.VMEM((2 * rows, width), full),
            pltpu.VMEM((2 * rows, width), full),
            pltpu.VMEM((3, rows, width), low),
            pltpu.VMEM((3, rows, width), low),
            dma((sems,)),
            dma((sems,)),
            dma((1 + outer + 2 + outer,)),
        ],
        compiler_params=pltpu.CompilerParams(
            vmem_limit_bytes=60 << 20, collective_id=2, has_side_effects=True
        ),
        cost_estimate=pl.CostEstimate(
            flops=13 << 30, bytes_accessed=30 << 20, transcendentals=rows * hidden * 2
        ),
    )(att_low, w_out, w_up, w_down, tokens, cotangent, *biases)


def backward_kernel(shards, chips, heads, *refs):
    outer = shards // 2
    refs = list(refs)

    def take(count):
        got = refs[:count]
        del refs[:count]
        return got

    (p_down, p_up, p_out, mix, half_out, qkv, att, lse, h1_far, g_qkv) = take(10)
    (tokens, grad_mid, gain, sums_in, up_sums) = take(5)
    (t_down, o_up, t_out, qkv_out, grad_tokens, vec_out) = take(6)
    (c_down,) = take(1)
    b_up, b_out, b_qkv = [take(7) for _ in range(3)]
    (i_down, i_up, i_out, t_up, o_qkv) = take(5)
    (h1, datt_send, datt, keys_acc, values_acc, d_pos, d_st, p_qkv) = take(8)
    (side_send, lines, passed) = take(3)
    (vbuf, v_wt, v_own, v_core, v_z) = take(5)
    (sends, recvs, loads) = take(3)

    me, z, core = lax.axis_index("wt"), lax.axis_index("z"), lax.axis_index("core")
    devices = 2 * chips
    cols = heads * HEAD_DIM
    length = qkv.shape[0]
    block = length // (2 * devices)
    width = tokens.shape[1]
    shard = width // shards
    mine = z * 2 + core
    ids = Counter(sends, recvs)
    per_load = 2 + outer - 1
    scatters = [
        Scatter(part, bufs, ids, loads.at[pl.ds(i * per_load, per_load)], shards, me)
        for i, (part, bufs) in enumerate(
            ((p_up, b_up), (p_out, b_out), (p_qkv, b_qkv))
        )
    ]
    chains = [
        Chain(own, inbox, total, ids, pieces, chips, z, core)
        for own, inbox, total, pieces in zip(
            (c_down, b_up[0], b_out[0]), (i_down, i_up, i_out), (t_down, t_up, t_out), PIECES
        )
    ]
    s_datt = ids.take(4 * chips)
    r_datt = s_datt
    s_side = ids.take(chips)
    s_line = ids.take(2 * chips * LINE_CUTS)
    s_ring = ids.take(2 * (chips + 1))
    s_sib = ids.take(chips)
    s_vwt = ids.take(shards)
    s_vcore = ids.take(1)
    s_vz = ids.take(chips)

    def h1_load(s):
        at = pl.ds(pl.multiple_of(s * shard, shard), shard)
        slot = lax.rem(s, 2)
        return pltpu.make_async_copy(
            h1_far.at[:, :, at], h1.at[slot], loads.at[4 * per_load + slot]
        )

    @pl.loop(0, 2)
    def _(s):
        h1_load(s).start()

    down_load = pltpu.make_async_copy(p_down, c_down, loads.at[4 * per_load + 2])
    down_load.start()
    for scatter in scatters[:2]:
        for step in scatter.local_copies():
            step.start()
    greet(all_peers(shards, chips, me, z, core))
    scatters[0].start_first()
    scatters[0].start_early()
    down_load.wait()

    def datt_copy(chip, place, src_chip):
        low = place % 2 == 0
        c = 2 * src_chip + place // 2
        at = pl.multiple_of((c if low else 2 * devices - 1 - c) * block, block)
        return remote(
            datt_send.at[chip, pl.ds(place * block, block)],
            datt.at[pl.ds(at, block)],
            sends.at[s_datt + chip * 4 + place],
            recvs.at[r_datt + src_chip * 4 + place],
            z=chip,
        ), at

    @pl.loop(0, chips)
    def _(chip):
        rows_out = half_out[pl.ds(pl.multiple_of(chip * cols, cols), cols), :]
        datt_send[chip] = product_right(mix[...], rows_out).astype(jnp.bfloat16)

        @pl.when(chip != z)
        def _():
            for place in range(4):
                datt_copy(chip, place, z)[0].start()

        @pl.when(chip == z)
        def _():
            for place in range(4):
                at = datt_copy(chip, place, z)[1]
                datt[pl.ds(at, block)] = datt_send[chip, place * block : (place + 1) * block]

    keys_acc[...] = jnp.zeros_like(keys_acc)
    values_acc[...] = jnp.zeros_like(values_acc)

    @pl.loop(0, chips)
    def _(chip):
        @pl.when(chip != z)
        def _():
            for place in range(4):
                copy, at = datt_copy(chip, place, chip)
                copy.wait_recv()

    scale = HEAD_DIM ** (-0.5)

    @pl.loop(0, 2 * chips)
    def _(i):
        q_start = pl.multiple_of(i * Q_TILE, Q_TILE)
        q_rows = pl.ds(q_start, Q_TILE)
        queries, grads, norms, deltas = [], [], [], []
        for h in range(heads):
            at = slice(h * HEAD_DIM, (h + 1) * HEAD_DIM)
            queries.append(qkv[q_rows, at] * jnp.bfloat16(scale))
            grad = datt[q_rows, at]
            grads.append(grad)
            norms.append(lse[q_rows, h : h + 1])
            deltas.append(
                jnp.sum(grad.astype(jnp.float32) * att[q_rows, at], axis=-1, keepdims=True)
            )

        def step(masked, j, carried):
            k_start = pl.multiple_of(j * K_TILE, K_TILE)
            k_rows = pl.ds(k_start, K_TILE)
            new = []
            for h in range(heads):
                own = slice(h * HEAD_DIM, (h + 1) * HEAD_DIM)
                at = cols + h * HEAD_DIM
                keys = qkv[k_rows, at : at + HEAD_DIM]
                values = qkv[k_rows, at + cols : at + cols + HEAD_DIM]
                scores = product_right(queries[h], keys)
                if masked:
                    scores = jnp.where(tile_allowed(q_start, k_start), scores, MASKED_SCORE)
                prob = jnp.exp(scores - norms[h])
                grad_prob = product_right(grads[h], values)
                grad_score = (prob * (grad_prob - deltas[h])).astype(jnp.bfloat16)
                values_acc[k_rows, own] += product_left(prob.astype(jnp.bfloat16), grads[h])
                keys_acc[k_rows, own] += product_left(grad_score, queries[h])
                new.append(carried[h] + product(grad_score, keys))
            return tuple(new)

        steps = (q_start + Q_TILE + K_TILE - 1) // K_TILE
        zero = jnp.zeros((Q_TILE, HEAD_DIM), jnp.float32)
        done = lax.fori_loop(0, steps - 1, functools.partial(step, False), (zero,) * heads)
        done = step(True, steps - 1, done)
        for h in range(heads):
            d_pos[q_rows, h * HEAD_DIM : (h + 1) * HEAD_DIM] = (done[h] * scale).astype(
                jnp.bfloat16
            )

        chains[0].wave(i)

        @pl.when(i == chips)
        def _():
            scatters[0].start_late()
            scatters[1].start_first()
            scatters[1].start_early()

    d_pos[:, cols : 2 * cols] = keys_acc[...].astype(jnp.bfloat16)
    d_pos[:, 2 * cols :] = values_acc[...].astype(jnp.bfloat16)

    @pl.loop(0, devices)
    def _(slot):
        d_st[slot, :block] = d_pos[pl.ds(slot * block, block), :]
        d_st[slot, block:] = d_pos[pl.ds((2 * devices - 1 - slot) * block, block), :]

    def side(chip):
        return remote(
            side_send.at[chip],
            lines.at[chip],
            sends.at[s_side + chip],
            recvs.at[s_side + chip],
            core=1 - core,
        )

    @pl.loop(0, chips)
    def _(chip):
        side_send[chip] = product_right(d_st[chip * 2 + 1 - core], g_qkv[...]).astype(jnp.bfloat16)
        side(chip).start()

    @pl.loop(0, chips)
    def _(chip):
        part = product_right(d_st[chip * 2 + core], g_qkv[...])
        side(chip).wait_recv()
        lines[chip] = (part + lines[chip].astype(jnp.float32)).astype(jnp.bfloat16)

    sub = block * 2 // LINE_CUTS

    def line_copy(way, chip, cut):
        at = pl.ds(pl.multiple_of(cut * sub, sub), sub)
        sem = s_line + (way * chips + chip) * LINE_CUTS + cut
        return remote(
            lines.at[chip, at],
            passed.at[chip + 1 - way, at],
            sends.at[sem],
            recvs.at[sem],
            z=z - 1 if way else z + 1,
        )

    def line_wave(turn):
        for way in range(2):
            hops = chips - 1 - z if way else z
            part = turn - hops
            clipped = jnp.maximum(part, 0)
            far, cut = clipped // LINE_CUTS, lax.rem(clipped, LINE_CUTS)
            chip = far if way else chips - 1 - far
            ahead = chip < z if way else chip > z

            @pl.when((part >= 0) & ahead)
            def _():
                copy = line_copy(way, chip, cut)

                @pl.when(hops > 0)
                def _():
                    at = pl.ds(pl.multiple_of(cut * sub, sub), sub)
                    copy.wait_recv()
                    add_rows(lines.at[chip, at], [passed.at[chip + 1 - way, at]])

                copy.start()

    line_turns = (chips - 1) * LINE_CUTS
    line_wave(0)
    scatters[1].start_late()
    scatters[0].finish()
    tiles = 2 * chips

    def waves(turn):
        line_wave(turn + 1)
        chains[0].wave(turn + tiles)
        chains[1].wave(turn)
        chains[2].wave(turn - shards)


    @pl.loop(0, shards)
    def _(s):
        h1_load(s).wait()
        side_of = lax.rem(s, 2)

        def part(slot, total):
            return total + product_left(h1[side_of, slot], d_st[slot])

        total = lax.fori_loop(0, devices, part, jnp.zeros((shard, 3 * cols), jnp.float32))
        p_qkv[s] = total.astype(jnp.bfloat16)

        @pl.when(s + 2 < shards)
        def _():
            h1_load(s + 2).start()

        waves(s)

    for step in scatters[2].local_copies():
        step.start()
    scatters[2].start_first()
    scatters[2].start_early()
    scatters[1].finish()
    done = max(shards + chips - 2, line_turns)
    pl.loop(shards, done)(waves)
    scatters[2].start_late()

    early = done + 3
    pl.loop(done, early)(waves)

    vbuf[...] = jnp.zeros_like(vbuf)
    share = up_sums.shape[1] // shards
    for s in range(shards):
        vbuf[s, 2:6, :] = sums_in[0:4, s * shard : (s + 1) * shard]
        for c in range(2):
            for r in range(share // shard):
                at = s * share + r * shard
                row = 6 + c * (share // shard) + r
                vbuf[s, row : row + 1, :] = jnp.where(core == c, up_sums[:, at : at + shard], 0.0)
    sums = jnp.sum(d_st[...].reshape(length, 3 * cols).astype(jnp.float32), axis=0, keepdims=True)
    per_shard = vbuf.shape[2] // cols
    bias_shard, bias_row = mine // per_shard, lax.rem(mine, per_shard)
    for row in range(per_shard):
        own_row = bias_row == row
        vbuf[bias_shard, 10 + row : 11 + row, :cols] = jnp.where(own_row, sums[:, :cols], 0.0)
        row += per_shard
        vbuf[bias_shard, 10 + row : 11 + row, :cols] = jnp.where(own_row, sums[:, 2 * cols :], 0.0)

    for cut in range(LINE_CUTS):

        @pl.when(z > 0)
        def _():
            line_copy(0, z, cut).wait_recv()

        @pl.when(z < chips - 1)
        def _():
            line_copy(1, z, cut).wait_recv()

    left_part = jnp.where(z > 0, passed[z + 1].astype(jnp.float32), 0.0)
    right_part = jnp.where(z < chips - 1, passed[z].astype(jnp.float32), 0.0)
    dh1 = lines[z].astype(jnp.float32) + left_part + right_part
    values_in = tokens[...].astype(jnp.float32)
    centred = values_in - jnp.mean(values_in, axis=-1, keepdims=True)
    spread = lax.rsqrt(jnp.mean(centred * centred, axis=-1, keepdims=True) + EPSILON)
    normal = centred * spread
    inner = dh1 * gain[...]
    grad_tokens[...] = grad_mid[...] + spread * (
        inner
        - jnp.mean(inner, axis=-1, keepdims=True)
        - normal * jnp.mean(inner * normal, axis=-1, keepdims=True)
    )
    gain_sum = jnp.sum(dh1 * normal, axis=0, keepdims=True)
    shift_sum = jnp.sum(dh1, axis=0, keepdims=True)
    for s in range(shards):
        vbuf[s, 0:1, :] = gain_sum[:, s * shard : (s + 1) * shard]
        vbuf[s, 1:2, :] = shift_sum[:, s * shard : (s + 1) * shard]

    def v_copy(k):
        slot = lax.rem(me + k, shards)
        return remote(
            vbuf.at[slot], v_wt.at[k], sends.at[s_vwt + k], recvs.at[s_vwt + k], wt=slot
        )

    for k in range(1, shards):
        v_copy(k).start()

    scatters[2].finish()
    got = b_qkv[0]

    def right(slot, d):
        sem = s_ring + d
        return remote(o_qkv.at[slot], o_qkv.at[slot], sends.at[sem], recvs.at[sem], z=z + 1)

    def left(slot, d):
        sem = s_ring + chips + 1 + d
        return remote(o_qkv.at[slot], o_qkv.at[slot], sends.at[sem], recvs.at[sem], z=z - 1)

    def sibling(chip, of):
        slot = chip * 2 + of
        sem = s_sib + chip
        return remote(o_qkv.at[slot], o_qkv.at[slot], sends.at[sem], recvs.at[sem], core=1 - core)

    o_qkv[mine] = got[...]

    @pl.when(z + 1 < chips)
    def _():
        right(mine, 1).start()

    @pl.when(z > 0)
    def _():
        left(mine, 1).start()

    sibling(z, core).start()
    pl.loop(early, chains[2].waves() + shards)(waves)

    total = vbuf[me]
    for k in range(1, shards):
        v_copy(k).wait_recv()
        total = total + v_wt[k]
    v_own[...] = total
    v_swap = remote(v_own, v_core, sends.at[s_vcore], recvs.at[s_vcore], core=1 - core)
    v_swap.start()
    v_swap.wait_recv()
    v_z[z] = v_own[...] + v_core[...]

    def vz_copy(chip, src):
        return remote(
            v_z.at[src], v_z.at[src], sends.at[s_vz + chip], recvs.at[s_vz + src], z=chip
        )

    @pl.loop(0, chips)
    def _(chip):
        @pl.when(chip != z)
        def _():
            vz_copy(chip, z).start()

    for d in range(1, chips):

        @pl.when(z >= d)
        def _():
            slot = (z - d) * 2 + core
            right(slot, d).wait_recv()

            @pl.when(z + 1 < chips)
            def _():
                right(slot, d + 1).start()

            sibling(z - d, core).start()

        @pl.when(z + d < chips)
        def _():
            slot = (z + d) * 2 + core
            left(slot, d).wait_recv()

            @pl.when(z > 0)
            def _():
                left(slot, d + 1).start()

            sibling(z + d, core).start()

    @pl.loop(0, chips)
    def _(chip):
        @pl.when(chip != z)
        def _():
            vz_copy(chip, chip).wait_recv()

    vec_total = v_z[0]
    for chip in range(1, chips):
        vec_total = vec_total + v_z[chip]
    vec_out[...] = vec_total

    for chain in chains:
        chain.finish()
    share = t_up.shape[2] // shards
    for c in range(2):
        for s in range(shards):
            o_up[:, (2 * s + c) * share : (2 * s + c + 1) * share] = t_up[
                c, :, s * share : (s + 1) * share
            ]

    @pl.loop(0, chips)
    def _(chip):
        sibling(chip, 1 - core).wait_recv()

    for slot in range(devices):
        for third in range(3):
            at = third * width + slot * cols
            qkv_out[:, at : at + cols] = o_qkv[slot, :, third * cols : (third + 1) * cols]

    for scatter in scatters:
        scatter.sent()

    @pl.loop(0, chips)
    def _(chip):
        side(chip).wait_send()
        sibling(chip, core).wait_send()

        @pl.when(chip != z)
        def _():
            vz_copy(chip, z).wait_send()
            for place in range(4):
                datt_copy(chip, place, z)[0].wait_send()

    for k in range(1, shards):
        v_copy(k).wait_send()
    v_swap.wait_send()
    @pl.loop(0, chips)
    def _(chip):
        for cut in range(LINE_CUTS):

            @pl.when(z < chip)
            def _():
                line_copy(0, chip, cut).wait_send()

            @pl.when(z > chip)
            def _():
                line_copy(1, chip, cut).wait_send()

    for d in range(1, chips + 1):

        @pl.when((z + 1 < chips) & (z - d + 1 >= 0))
        def _():
            right((z - d + 1) * 2 + core, d).wait_send()

        @pl.when((z > 0) & (z + d - 1 < chips))
        def _():
            left((z + d - 1) * 2 + core, d).wait_send()


def backward(p_down, p_up, p_out, mix, half_out, qkv, att, lse, h1, g_qkv, tokens, grad_mid,
             gain, sums, up_sums, shards, chips, heads):
    outer = shards // 2
    cols = heads * HEAD_DIM
    rows, width = tokens.shape
    length = qkv.shape[0]
    vmem = pl.BlockSpec(memory_space=pltpu.VMEM)
    hbm = pl.BlockSpec(memory_space=pl.ANY)
    low, full = jnp.bfloat16, jnp.float32
    shape = jax.ShapeDtypeStruct
    dma = pltpu.SemaphoreType.DMA
    shard = width // shards
    sizes = [p_down.shape] + [p.shape[1:] for p in (p_up, p_out)]
    scatter = [pltpu.VMEM(p_down.shape, low)]
    for size in sizes[1:] + [(shard, 3 * cols)]:
        scatter += Scatter.scratch(outer, *size)
    far = outer - 1
    sems = (
        4 * (2 + 4 * far)
        + 6 * sum(PIECES)
        + 4 * chips + chips + 2 * chips * LINE_CUTS + 2 * (chips + 1) + chips + shards + 1 + chips
    )
    vec_shape = (VEC_ROWS, shard)
    return pl.pallas_call(
        functools.partial(backward_kernel, shards, chips, heads),
        in_specs=[hbm] * 3 + [vmem] * 5 + [hbm] + [vmem] * 6,
        out_specs=[vmem] * 6,
        out_shape=[
            shape((2,) + sizes[0], low),
            shape((sizes[1][0], 2 * sizes[1][1]), low),
            shape((2,) + sizes[2], low),
            shape((shard, 3 * width), low),
            shape((rows, width), full),
            shape(vec_shape, full),
        ],
        scratch_shapes=scatter
        + [pltpu.VMEM(size, low) for size in sizes]
        + [
            pltpu.VMEM((2,) + sizes[1], low),
            pltpu.VMEM((2 * chips, shard, 3 * cols), low),
            pltpu.VMEM((2,) + h1.shape[:2] + (shard,), low),
            pltpu.VMEM((chips, 2 * rows, cols), low),
            pltpu.VMEM((length, cols), low),
            pltpu.VMEM((length, cols), full),
            pltpu.VMEM((length, cols), full),
            pltpu.VMEM((length, 3 * cols), low),
            pltpu.VMEM((2 * chips, rows, 3 * cols), low),
            pltpu.VMEM((shards, shard, 3 * cols), low),
        ]
        + [pltpu.VMEM((chips + extra, rows, width), low) for extra in (0, 0, 1)]
        + [
            pltpu.VMEM((shards,) + vec_shape, full),
            pltpu.VMEM((shards,) + vec_shape, full),
            pltpu.VMEM(vec_shape, full),
            pltpu.VMEM(vec_shape, full),
            pltpu.VMEM((chips,) + vec_shape, full),
            dma((sems,)),
            dma((sems,)),
            dma((4 * (2 + far) + 3,)),
        ],
        compiler_params=pltpu.CompilerParams(
            vmem_limit_bytes=60 << 20, collective_id=1, has_side_effects=True
        ),
        cost_estimate=pl.CostEstimate(
            flops=20 << 30, bytes_accessed=50 << 20, transcendentals=length * length
        ),
    )(p_down, p_up, p_out, mix, half_out, qkv, att, lse, h1, g_qkv, tokens, grad_mid, gain, sums,
      up_sums)


def swap(value):
    return lax.ppermute(value, "core", [(0, 1), (1, 0)])


def pair_stack(own, core):
    other = swap(own)
    first = core == 0
    return jnp.stack([jnp.where(first, own, other), jnp.where(first, other, own)])


def pair_sum(partial, core):
    own = lax.dynamic_index_in_dim(partial, core, 0, keepdims=False)
    other = lax.dynamic_index_in_dim(partial, 1 - core, 0, keepdims=False)
    return own + swap(other.astype(jnp.bfloat16)).astype(jnp.float32)


def per_device(
    tokens,
    cotangent,
    ln1_gain,
    ln1_bias,
    w_qkv,
    bias_q,
    bias_v,
    w_out,
    bias_out,
    ln2_gain,
    ln2_bias,
    w_up,
    bias_up,
    w_down,
    bias_down,
):
    core = lax.axis_index("core")
    shards = lax.axis_size("wt")
    chips = lax.axis_size("z")
    devices = 2 * chips
    inputs_low = tokens[0]
    tok_count, width = inputs_low.shape
    half = width // 2
    shard = width // shards
    hidden = w_up.shape[1] // 2
    heads = HEADS // devices
    cols = heads * HEAD_DIM

    def pick(value):
        return lax.dynamic_index_in_dim(value, core, 1, keepdims=False)

    place = lax.axis_index("z")
    per_shard = shard // cols

    def head_rows(value):
        value = value.reshape(per_shard, cols)
        return jnp.pad(value, ((0, 0), (0, shard - cols)))

    vec = jnp.concatenate(
        [
            jnp.stack([ln1_gain, ln1_bias, bias_out, ln2_gain, ln2_bias, bias_down]),
            bias_up.reshape(4, shard),
            head_rows(bias_q),
            head_rows(bias_v),
            jnp.zeros((VEC_ROWS - 10 - 2 * per_shard, shard), jnp.bfloat16),
        ]
    ).astype(jnp.float32)
    own_qkv = w_qkv.reshape(shard, 3, devices, cols)
    own_qkv = lax.dynamic_index_in_dim(own_qkv, place * 2 + core, 2, keepdims=False)
    vecs, h1_all, qkv, attended, log_norm, att_back, g_qkv, g_out, g_up, g_down = forward(
        inputs_low, vec, own_qkv.reshape(shard, 3 * cols), w_out, w_up, w_down, shards, chips, heads
    )
    gain_one, shift_one, out_bias, gain_two, shift_two, down_bias = [
        vecs[:, i].reshape(-1) for i in range(6)
    ]
    up_bias = pick(vecs[:, 6:10].reshape(shards, 2, -1)).reshape(-1)
    half_qkv = g_qkv.reshape(width, 3 * cols)
    half_out = g_out.reshape(half, width)
    biases = [v.reshape(1, -1) for v in (out_bias, gain_two, shift_two, down_bias, up_bias)]
    out, grad_mid, mix_pair, grad_up, grad_out, red_down, sums, up_sums = feed(
        att_back,
        half_out,
        g_up.reshape(width, hidden),
        g_down,
        inputs_low,
        cotangent[0],
        biases,
        shards,
        chips,
    )

    down_all, up_all, out_all, qkv_all, grad_inputs, vector = backward(
        red_down,
        grad_up.reshape(shards, shard, hidden),
        grad_out.reshape(shards, -1, width),
        mix_pair.reshape(2 * tok_count, width),
        half_out,
        qkv,
        attended,
        log_norm,
        h1_all,
        half_qkv,
        inputs_low,
        grad_mid,
        gain_one.reshape(1, width),
        sums,
        up_sums,
        shards,
        chips,
        heads,
    )
    full = jnp.float32
    grad_inputs = grad_inputs[None]
    down_out = down_all.reshape(-1, width).astype(full)
    up_out = up_all.astype(full)
    out_out = jnp.moveaxis(out_all.reshape(2, -1, cols, width), 0, 1).reshape(-1, width)
    out_out = out_out.astype(full)
    qkv_out = qkv_all.astype(full)
    rows_q = vector[10 : 10 + per_shard, :cols].reshape(-1)
    rows_v = vector[10 + per_shard : 10 + 2 * per_shard, :cols].reshape(-1)
    vector_out = [
        vector[0], vector[1], rows_q, rows_v, vector[2], vector[3], vector[4], vector[5],
        vector[6:10].reshape(-1),
    ]
    return (
        out[None],
        grad_inputs,
        vector_out[0],
        vector_out[1],
        qkv_out,
        vector_out[2],
        vector_out[3],
        out_out,
        vector_out[4],
        vector_out[5],
        vector_out[6],
        up_out,
        vector_out[8],
        down_out,
        vector_out[7],
    )


def solution(mesh):
    count = mesh.shape["ctx"]
    split = Mesh(
        np.asarray(mesh.devices).reshape(count // 2, 2, mesh.shape["wt"]), ("z", "core", "wt")
    )
    return jax.shard_map(
        per_device,
        mesh=split,
        in_specs=(
            P("wt", ("z", "core"), None),
            P("wt", ("z", "core"), None),
            P("wt"),
            P("wt"),
            P("wt", None),
            P("wt"),
            P("wt"),
            P("wt", None),
            P("wt"),
            P("wt"),
            P("wt"),
            P("wt", None),
            P("wt"),
            P("wt", None),
            P("wt"),
        ),
        out_specs=(
            P("wt", ("z", "core"), None),
            P("wt", ("z", "core"), None),
            P("wt"),
            P("wt"),
            P("wt", None),
            P("wt"),
            P("wt"),
            P("wt", None),
            P("wt"),
            P("wt"),
            P("wt"),
            P("wt", None),
            P("wt"),
            P("wt", None),
            P("wt"),
        ),
        check_vma=False,
    )
```
